32 devices in a mesh: dp: 4 (over y, core), mp: 8 (over z, x).
Axes of the slice: x: 2, y: 2, z: 4, core: 2. Of those that a mesh axis runs over, the one named last changes fastest.
Arguments:
- student_rows: bfloat16 [3072, 256], P('dp'), may hold values from -12 to 12
- teacher_rows: bfloat16 [3072, 256], P('dp'), may hold values from -12 to 12
- student_protos: bfloat16 [256, 65536], P(None, 'mp'), may hold values from -12 to 12
- teacher_protos: bfloat16 [256, 65536], P(None, 'mp'), may hold values from -12 to 12
- center: float32 [65536], P('mp'), may hold values from -0.25 to 0.25
- row_weight: float32 [3072], P('dp'), may hold values from 0.25 to 4
Outputs:
- grad_rows: float32 [3072, 256], P('dp')
- proto_grad: float32 [256, 65536], P('dp', 'mp')
The draws below stay inside these ranges and needn't reach their ends.
All inputs are finite; a program needn't handle non-finite values.
Results may differ from the reference program's by a relative error of at most 0.012.
The reference program's roundings to bfloat16 on the way (of `z_student`, `z_teacher`, `w_student`, `w_teacher` and `grad_logit`) count: a program that leaves them out, or rounds other values in their place, can miss the bound.
Values sent between devices are 32-bit elements; how exact they have to be, the bound alone decides.
A program may use at most 192 MiB of HBM per device.

```python
import math
import jax
import jax.numpy as jnp
from jax import lax

B = 256
K = 65536
ROWS = 3072


def feature_scales(key):
    low = math.log(0.05)
    high = math.log(2.0)
    return jnp.exp(jax.random.uniform(jax.random.fold_in(key, 11), (B,), jnp.float32, low, high))


def base_values(key, shape):
    return jax.random.normal(key, shape, jnp.float32)


def row_base(key):
    values = base_values(jax.random.fold_in(key, 23), (ROWS, B))
    return values


def proto_base(key):
    return base_values(jax.random.fold_in(key, 31), (B, K))


def draw_student_rows(key, part):
    values = row_base(key) * feature_scales(key)[None, :]
    return jnp.clip(values, -12.0, 12.0).astype(jnp.bfloat16)


def draw_teacher_rows(key, part):
    noise = jax.random.normal(jax.random.fold_in(key, 29), (ROWS, B), jnp.float32)
    values = (row_base(key) + 0.6 * noise) * feature_scales(key)[None, :]
    return jnp.clip(values, -12.0, 12.0).astype(jnp.bfloat16)


def draw_student_protos(key, part):
    values = proto_base(key) * feature_scales(key)[:, None]
    return jnp.clip(values, -12.0, 12.0).astype(jnp.bfloat16)


def draw_teacher_protos(key, part):
    noise = jax.random.normal(jax.random.fold_in(key, 37), (B, K), jnp.float32)
    values = (proto_base(key) + 0.3 * noise) * feature_scales(key)[:, None]
    return jnp.clip(values, -12.0, 12.0).astype(jnp.bfloat16)


def steps_of(rng, dims, pieces, low, high):
    loudness = 1.0
    for position, shards_of in pieces:
        steps = jax.random.uniform(jax.random.fold_in(jax.random.fold_in(rng, 6), position), (shards_of,), jnp.float32, low / len(pieces), high / len(pieces))
        loudness = loudness * jnp.repeat(jnp.exp(steps), dims[position] // shards_of).reshape((-1,) + (1,) * (len(dims) - 1 - position))
    return loudness


def scatter_about(own_key, dims, scale, reach, cuts=(), kind=jnp.bfloat16):
    entries = jax.random.normal(own_key, dims, jnp.float32) * scale
    if len(cuts) > 0:
        entries = steps_of(own_key, dims, cuts, -0.22, 0.18) * entries
    return jnp.clip(entries, min=-reach, max=reach).astype(kind)


def setup_inputs(seed: int = 0) -> dict:
    splits = jax.random.split(jax.random.key(seed), 7)
    student_rows = draw_student_rows(jax.random.fold_in(splits[6], 71), 0)
    teacher_rows = draw_teacher_rows(jax.random.fold_in(splits[6], 71), 0)
    student_protos = draw_student_protos(jax.random.fold_in(splits[6], 71), 0)
    teacher_protos = draw_teacher_protos(jax.random.fold_in(splits[6], 71), 0)
    center = scatter_about(splits[4], (K,), 0.05, 0.25, ((0, 8),), jnp.float32)
    row_weight = jnp.clip(jnp.exp(math.log(4.0) - 2.7725887 * jax.random.uniform(splits[5], (ROWS,), jnp.float32) ** steps_of(splits[5], (ROWS,), ((0, 4),), -0.2, 0.2)), 0.25, 4.0)
    return {"student_rows": student_rows, "teacher_rows": teacher_rows, "student_protos": student_protos, "teacher_protos": teacher_protos, "center": center, "row_weight": row_weight}


student_temp = 0.1
teacher_temp = 0.04
norm_eps = 1e-06

def reference(student_rows, teacher_rows, student_protos, teacher_protos, center, row_weight):
    s_full = student_rows.astype(jnp.float32)
    row_norm = jnp.sqrt(lax.optimization_barrier(jnp.sum(s_full * s_full, axis=1, keepdims=True)) + norm_eps)
    z_unit = s_full / row_norm
    z_student = z_unit.astype(jnp.bfloat16)
    t_full = teacher_rows.astype(jnp.float32)
    z_teacher = (t_full / jnp.sqrt(lax.optimization_barrier(jnp.sum(t_full * t_full, axis=1, keepdims=True)) + norm_eps)).astype(jnp.bfloat16)
    v_full = student_protos.astype(jnp.float32)
    col_norm = jnp.sqrt(lax.optimization_barrier(jnp.sum(v_full * v_full, axis=0, keepdims=True)) + norm_eps)
    w_student = (v_full / col_norm).astype(jnp.bfloat16)
    u_full = teacher_protos.astype(jnp.float32)
    w_teacher = (u_full / jnp.sqrt(lax.optimization_barrier(jnp.sum(u_full * u_full, axis=0, keepdims=True)) + norm_eps)).astype(jnp.bfloat16)
    total_rows = student_rows.shape[0]
    block = math.gcd(total_rows, 512)
    blocks = total_rows // block

    def one_block(grad_w, index):
        start = (index * block).astype(jnp.int32)
        zs_block = lax.dynamic_slice_in_dim(z_student, start, block, 0)
        zt_block = lax.dynamic_slice_in_dim(z_teacher, start, block, 0)
        weights = lax.dynamic_slice_in_dim(row_weight, start, block, 0)
        s_logit = jnp.dot(zs_block, w_student, preferred_element_type=jnp.float32)
        t_logit = jnp.dot(zt_block, w_teacher, preferred_element_type=jnp.float32)
        e_student = jnp.exp((s_logit - 1.0) / student_temp)
        e_teacher = jnp.exp((t_logit - center[None, :] - 1.0) / teacher_temp)
        sum_student = lax.optimization_barrier(jnp.sum(e_student, axis=1, keepdims=True))
        sum_teacher = lax.optimization_barrier(jnp.sum(e_teacher, axis=1, keepdims=True))
        grad_logit = (weights[:, None] * (e_student / sum_student - e_teacher / sum_teacher) / student_temp).astype(jnp.bfloat16)
        grad_unit = jnp.dot(grad_logit, w_student.T, preferred_element_type=jnp.float32)
        grad_w = grad_w + jnp.dot(zs_block.T, grad_logit, preferred_element_type=jnp.float32)
        return (grad_w, grad_unit)
    grad_w, stacked = lax.scan(one_block, jnp.zeros(student_protos.shape, jnp.float32), jnp.arange(blocks, dtype=jnp.int32))
    grad_unit = stacked.reshape(total_rows, student_rows.shape[1])
    grad_rows = (grad_unit - z_unit * lax.optimization_barrier(jnp.sum(z_unit * grad_unit, axis=1, keepdims=True))) / row_norm
    w_float = w_student.astype(jnp.float32)
    col_dot = lax.optimization_barrier(jnp.sum(w_float * grad_w, axis=0, keepdims=True))
    proto_grad = (grad_w - w_float * col_dot) / col_norm
    return (grad_rows, proto_grad)
```

```python
import functools
import math

import jax
import jax.numpy as jnp
from jax import lax
from jax.experimental import pallas as pl
from jax.experimental.pallas import tpu as pltpu
from jax.sharding import PartitionSpec as P

student_temp = 0.1
teacher_temp = 0.04
norm_eps = 1e-06
MESH = pl.DeviceIdType.MESH
LOG2E = math.log2(math.e)
LANES = 128
LAG = 3


def kernel(n_dp, n_mp, tile,
           rs_ref, rt_ref, ps_hbm, pt_hbm, ctr_ref, wt_ref,
           rows_out, protos_hbm,
           ps, pt, e_s, e_t, zs, zt, zst, inv_col, inv_row, z_unit, acc_s, acc_t, sums, sums_in,
           gu, gu_in, gu_all, part, core_in, chip_in,
           load_sem, sum_sem, core_sem, chip_sem, store_sem, rs_sem, ag_sem):
    rows, feats = rs_ref.shape
    steps = ps.shape[0]
    groups = n_dp // 2
    block = feats // n_dp
    piece = rows // n_mp
    dp, mp = lax.axis_index("dp"), lax.axis_index("mp")
    group, core = dp // 2, dp % 2
    other = 1 - core

    def load(i, which):
        cols = pl.ds(pl.multiple_of(i * tile, tile), tile)
        src, dst = ((ps_hbm, ps), (pt_hbm, pt))[which]
        return pltpu.make_async_copy(src.at[:, cols], dst.at[i], load_sem.at[which, i])

    def load_start(i, _):
        load(i, 0).start()
        load(i, 1).start()
        return 0

    lax.fori_loop(0, steps, load_start, 0)

    barrier = pltpu.get_barrier_semaphore()
    pl.semaphore_signal(barrier, inc=1, device_id={"dp": group * 2 + other}, device_id_type=MESH)
    for d in range(1, groups):
        pl.semaphore_signal(
            barrier, inc=1, device_id={"dp": lax.rem(group + d, groups) * 2 + core}, device_id_type=MESH)
    for d in range(1, n_mp):
        pl.semaphore_signal(barrier, inc=1, device_id={"mp": lax.rem(mp + d, n_mp)}, device_id_type=MESH)

    x = rs_ref[...].astype(jnp.float32)
    r_inv = 1.0 / jnp.sqrt(jnp.sum(x * x, axis=1, keepdims=True) + norm_eps)
    zu = x * r_inv
    z_unit[...] = zu
    inv_row[...] = jnp.broadcast_to(r_inv, (rows, LANES))
    zs[...] = zu.astype(jnp.bfloat16)
    zst[...] = zu.T.astype(jnp.bfloat16)
    x = rt_ref[...].astype(jnp.float32)
    zt[...] = (x / jnp.sqrt(jnp.sum(x * x, axis=1, keepdims=True) + norm_eps)).astype(jnp.bfloat16)
    acc_s[...] = jnp.zeros_like(acc_s)
    acc_t[...] = jnp.zeros_like(acc_t)

    def lanes(e):
        return sum(e[:, k * LANES:(k + 1) * LANES] for k in range(tile // LANES))

    def forward(i, _):
        load(i, 0).wait()
        load(i, 1).wait()
        v = ps[i].astype(jnp.float32)
        c_inv = 1.0 / jnp.sqrt(jnp.sum(v * v, axis=0, keepdims=True) + norm_eps)
        inv_col[i] = c_inv
        w = (v * c_inv).astype(jnp.bfloat16)
        ps[i] = w
        s = jnp.dot(zs[...], w, preferred_element_type=jnp.float32)
        es = jnp.exp2((s - 1.0) * (LOG2E / student_temp))
        acc_s[...] += lanes(es)
        e_s[i] = es.astype(jnp.bfloat16)
        u = pt[i].astype(jnp.float32)
        u_inv = 1.0 / jnp.sqrt(jnp.sum(u * u, axis=0, keepdims=True) + norm_eps)
        wt = (u * u_inv).astype(jnp.bfloat16)
        t = jnp.dot(zt[...], wt, preferred_element_type=jnp.float32)
        shift = ctr_ref[:, pl.ds(pl.multiple_of(i * tile, tile), tile)] + 1.0
        et = jnp.exp2((t - shift) * (LOG2E / teacher_temp))
        acc_t[...] += lanes(et)
        e_t[i] = et.astype(jnp.bfloat16)
        return 0

    lax.fori_loop(0, steps, forward, 0)

    sums[0:1, :] = jnp.sum(acc_s[...].T, axis=0, keepdims=True)
    sums[1:2, :] = jnp.sum(acc_t[...].T, axis=0, keepdims=True)
    pl.semaphore_wait(barrier, 1 + (groups - 1) + (n_mp - 1))

    def sum_copy(d):
        return pltpu.make_async_remote_copy(
            src_ref=sums, dst_ref=sums_in.at[d], send_sem=sum_sem.at[0, d], recv_sem=sum_sem.at[1, d],
            device_id={"mp": lax.rem(mp + d, n_mp)}, device_id_type=MESH)

    for d in range(1, n_mp):
        sum_copy(d).start()
    total = sums[...]
    for d in range(1, n_mp):
        sum_copy(d).wait()
        total = total + sums_in[d]
    scale = wt_ref[...] / student_temp / total
    acc_s[...] = jnp.broadcast_to(scale[0:1, :], (LANES, rows)).T
    acc_t[...] = jnp.broadcast_to(scale[1:2, :], (LANES, rows)).T
    gu[...] = jnp.zeros_like(gu)

    def rows_of(q, c):
        return pl.ds(pl.multiple_of((q * 2 + c) * block, block), block)

    def core_copy(i, q):
        return pltpu.make_async_remote_copy(
            src_ref=part.at[i, rows_of(q, other)], dst_ref=core_in.at[i, q],
            send_sem=core_sem.at[0, i, q], recv_sem=core_sem.at[1, i, q],
            device_id={"dp": group * 2 + other}, device_id_type=MESH)

    def chip_copy(i, d):
        to = lax.rem(group + d, groups)
        return pltpu.make_async_remote_copy(
            src_ref=part.at[i, rows_of(to, core)], dst_ref=chip_in.at[i, d - 1],
            send_sem=chip_sem.at[0, i, d - 1], recv_sem=chip_sem.at[1, i, d - 1],
            device_id={"dp": to * 2 + core}, device_id_type=MESH)

    def forward_chip(i):
        for q in range(groups):
            core_copy(i, q).wait()
        for d in range(groups):
            q = lax.rem(group + d, groups)
            part[i, rows_of(q, core)] += core_in[i, q]
            if d:
                chip_copy(i, d).start()

    def wide(a):
        return jnp.concatenate([a] * (tile // LANES), axis=1)

    def backward(i, _):
        a = wide(acc_s[...]) * e_s[i].astype(jnp.float32)
        b = wide(acc_t[...]) * e_t[i].astype(jnp.float32)
        g = (a - b).astype(jnp.bfloat16)
        w = ps[i]
        gw = jnp.dot(zst[...], g, preferred_element_type=jnp.float32)
        wf = w.astype(jnp.float32)
        part[i] = (gw - wf * jnp.sum(wf * gw, axis=0, keepdims=True)) * inv_col[i]
        for q in range(groups):
            core_copy(i, q).start()
        gu[...] += lax.dot_general(g, w, (((1,), (1,)), ((), ())), preferred_element_type=jnp.float32)

        @pl.when(i >= LAG)
        def _():
            forward_chip(i - LAG)
        return 0

    lax.fori_loop(0, steps, backward, 0)

    g_all = gu[...]
    zu = z_unit[...]
    dots = jnp.sum(zu * g_all, axis=1, keepdims=True)
    gu[...] = (g_all - zu * dots) * inv_row[:, 0:1]

    def piece_of(j):
        return pl.ds(pl.multiple_of(j * piece, piece), piece)

    def rs_copy(d):
        to = lax.rem(mp + d, n_mp)
        return pltpu.make_async_remote_copy(
            src_ref=gu.at[piece_of(to)], dst_ref=gu_in.at[d], send_sem=rs_sem.at[0, d], recv_sem=rs_sem.at[1, d],
            device_id={"mp": to}, device_id_type=MESH)

    def ag_copy(d):
        return pltpu.make_async_remote_copy(
            src_ref=gu_in.at[0], dst_ref=gu_all.at[d], send_sem=ag_sem.at[0, d], recv_sem=ag_sem.at[1, d],
            device_id={"mp": lax.rem(mp + d, n_mp)}, device_id_type=MESH)

    for d in range(1, n_mp):
        rs_copy(d).start()

    def tail(i, _):
        forward_chip(i)
        return 0

    lax.fori_loop(max(steps - LAG, 0), steps, tail, 0)

    def store(i):
        cols = pl.ds(pl.multiple_of(i * tile, tile), tile)
        return pltpu.make_async_copy(part.at[i, rows_of(group, core)], protos_hbm.at[:, cols], store_sem.at[i])

    def drain(i, _):
        own = part[i, rows_of(group, core)]
        for d in range(1, groups):
            chip_copy(i, d).wait()
            own = own + chip_in[i, d - 1]
        part[i, rows_of(group, core)] = own
        store(i).start()
        return 0

    early = steps * 5 // 8
    lax.fori_loop(0, early, drain, 0)

    mine = gu[piece_of(mp)]
    for d in range(1, n_mp):
        rs_copy(d).wait()
        mine = mine + gu_in[d]
    gu_in[0] = mine
    for d in range(1, n_mp):
        ag_copy(d).start()
    rows_out[piece_of(mp)] = mine

    lax.fori_loop(early, steps, drain, 0)

    for d in range(1, n_mp):
        ag_copy(d).wait()
        rows_out[piece_of(lax.rem(mp - d + n_mp, n_mp))] = gu_all[d]

    def stored(i, _):
        store(i).wait()
        return 0

    lax.fori_loop(0, steps, stored, 0)


def solution(mesh):
    n_dp, n_mp = mesh.shape["dp"], mesh.shape["mp"]
    groups = n_dp // 2

    def local(student_rows, teacher_rows, student_protos, teacher_protos, center, row_weight):
        rows, feats = student_rows.shape
        cols = student_protos.shape[1]
        tile = math.gcd(cols, 256)
        steps = cols // tile
        block, piece = feats // n_dp, rows // n_mp
        f32, bf16 = jnp.float32, jnp.bfloat16
        vmem, anywhere = pl.BlockSpec(memory_space=pltpu.VMEM), pl.BlockSpec(memory_space=pl.ANY)
        dma = pltpu.SemaphoreType.DMA
        return pl.pallas_call(
            functools.partial(kernel, n_dp, n_mp, tile),
            name="head_backward",
            out_shape=(jax.ShapeDtypeStruct((rows, feats), f32), jax.ShapeDtypeStruct((block, cols), f32)),
            in_specs=[vmem, vmem, anywhere, anywhere, vmem, vmem],
            out_specs=(vmem, anywhere),
            scratch_shapes=[
                pltpu.VMEM((steps, feats, tile), bf16),
                pltpu.VMEM((steps, feats, tile), bf16),
                pltpu.VMEM((steps, rows, tile), bf16),
                pltpu.VMEM((steps, rows, tile), bf16),
                pltpu.VMEM((rows, feats), bf16),
                pltpu.VMEM((rows, feats), bf16),
                pltpu.VMEM((feats, rows), bf16),
                pltpu.VMEM((steps, 1, tile), f32),
                pltpu.VMEM((rows, LANES), f32),
                pltpu.VMEM((rows, feats), f32),
                pltpu.VMEM((rows, LANES), f32),
                pltpu.VMEM((rows, LANES), f32),
                pltpu.VMEM((2, rows), f32),
                pltpu.VMEM((n_mp, 2, rows), f32),
                pltpu.VMEM((rows, feats), f32),
                pltpu.VMEM((n_mp, piece, feats), f32),
                pltpu.VMEM((n_mp, piece, feats), f32),
                pltpu.VMEM((steps, feats, tile), f32),
                pltpu.VMEM((steps, groups, block, tile), f32),
                pltpu.VMEM((steps, groups - 1, block, tile), f32),
                dma((2, steps)),
                dma((2, n_mp)),
                dma((2, steps, groups)),
                dma((2, steps, groups - 1)),
                dma((steps,)),
                dma((2, n_mp)),
                dma((2, n_mp)),
            ],
            compiler_params=pltpu.CompilerParams(
                collective_id=0, has_side_effects=True, vmem_limit_bytes=67043328),
        )(student_rows, teacher_rows, student_protos, teacher_protos, center[None, :], row_weight[None, :])

    placed = (P("dp", None), P("dp", None), P(None, "mp"), P(None, "mp"), P("mp"), P("dp"))
    return jax.shard_map(
        local, mesh=mesh, in_specs=placed, out_specs=(P("dp", None), P("dp", "mp")), check_vma=False
    )
```

```python
import functools
import math

import jax
import jax.numpy as jnp
from jax import lax
from jax.experimental import pallas as pl
from jax.experimental.pallas import tpu as pltpu
from jax.sharding import PartitionSpec as P

student_temp = 0.1
teacher_temp = 0.04
norm_eps = 1e-06
MESH = pl.DeviceIdType.MESH
LOG2E = math.log2(math.e)
LANES = 128
LAG = 2


def kernel(n_dp, n_mp, tile,
           rs_ref, rt_ref, ps_hbm, pt_hbm, ctr_ref, wt_ref,
           rows_out, protos_hbm,
           ps, pt, e_s, e_t, zs, zt, zst, inv_col, inv_row, z_unit, acc_s, acc_t, sums, sums_in,
           gu, gu_in, gu_all, part, core_in, chip_in,
           load_sem, sum_sem, core_sem, chip_sem, store_sem, rs_sem, ag_sem):
    rows, feats = rs_ref.shape
    steps = ps.shape[0]
    groups = n_dp // 2
    block = feats // n_dp
    piece = rows // n_mp
    dp, mp = lax.axis_index("dp"), lax.axis_index("mp")
    group, core = dp // 2, dp % 2
    other = 1 - core

    def load(i, which):
        cols = pl.ds(pl.multiple_of(i * tile, tile), tile)
        src, dst = ((ps_hbm, ps), (pt_hbm, pt))[which]
        return pltpu.make_async_copy(src.at[:, cols], dst.at[i], load_sem.at[which, i])

    def load_start(i, _):
        load(i, 0).start()
        load(i, 1).start()
        return 0

    lax.fori_loop(0, steps, load_start, 0)

    barrier = pltpu.get_barrier_semaphore()
    pl.semaphore_signal(barrier, inc=1, device_id={"dp": group * 2 + other}, device_id_type=MESH)
    for d in range(1, groups):
        pl.semaphore_signal(
            barrier, inc=1, device_id={"dp": lax.rem(group + d, groups) * 2 + core}, device_id_type=MESH)
    for d in range(1, n_mp):
        pl.semaphore_signal(barrier, inc=1, device_id={"mp": lax.rem(mp + d, n_mp)}, device_id_type=MESH)

    x = rs_ref[...].astype(jnp.float32)
    r_inv = 1.0 / jnp.sqrt(jnp.sum(x * x, axis=1, keepdims=True) + norm_eps)
    zu = x * r_inv
    z_unit[...] = zu
    inv_row[...] = jnp.broadcast_to(r_inv, (rows, LANES))
    zs[...] = zu.astype(jnp.bfloat16)
    zst[...] = zu.T.astype(jnp.bfloat16)
    x = rt_ref[...].astype(jnp.float32)
    zt[...] = (x / jnp.sqrt(jnp.sum(x * x, axis=1, keepdims=True) + norm_eps)).astype(jnp.bfloat16)
    acc_s[...] = jnp.zeros_like(acc_s)
    acc_t[...] = jnp.zeros_like(acc_t)

    def lanes(e):
        return sum(e[:, k * LANES:(k + 1) * LANES] for k in range(tile // LANES))

    def forward(i, _):
        load(i, 0).wait()
        load(i, 1).wait()
        v = ps[i].astype(jnp.float32)
        c_inv = 1.0 / jnp.sqrt(jnp.sum(v * v, axis=0, keepdims=True) + norm_eps)
        inv_col[i] = c_inv
        w = (v * c_inv).astype(jnp.bfloat16)
        ps[i] = w
        s = jnp.dot(zs[...], w, preferred_element_type=jnp.float32)
        es = jnp.exp2(s * (LOG2E / student_temp))
        acc_s[...] += lanes(es)
        e_s[i] = es.astype(jnp.bfloat16)
        u = pt[i].astype(jnp.float32)
        u_inv = 1.0 / jnp.sqrt(jnp.sum(u * u, axis=0, keepdims=True) + norm_eps)
        wt = (u * u_inv).astype(jnp.bfloat16)
        t = jnp.dot(zt[...], wt, preferred_element_type=jnp.float32)
        shift = ctr_ref[:, pl.ds(pl.multiple_of(i * tile, tile), tile)] * (LOG2E / teacher_temp)
        et = jnp.exp2(t * (LOG2E / teacher_temp) - shift)
        acc_t[...] += lanes(et)
        e_t[i] = et.astype(jnp.bfloat16)
        return 0

    lax.fori_loop(0, steps, forward, 0)

    sums[0:1, :] = jnp.sum(acc_s[...].T, axis=0, keepdims=True)
    sums[1:2, :] = jnp.sum(acc_t[...].T, axis=0, keepdims=True)
    pl.semaphore_wait(barrier, 1 + (groups - 1) + (n_mp - 1))

    def sum_copy(d):
        return pltpu.make_async_remote_copy(
            src_ref=sums, dst_ref=sums_in.at[d], send_sem=sum_sem.at[0, d], recv_sem=sum_sem.at[1, d],
            device_id={"mp": lax.rem(mp + d, n_mp)}, device_id_type=MESH)

    for d in range(1, n_mp):
        sum_copy(d).start()
    total = sums[...]
    for d in range(1, n_mp):
        sum_copy(d).wait()
        total = total + sums_in[d]
    scale = wt_ref[...] / student_temp / total
    acc_s[...] = jnp.broadcast_to(scale[0:1, :], (LANES, rows)).T
    acc_t[...] = jnp.broadcast_to(scale[1:2, :], (LANES, rows)).T
    gu[...] = jnp.zeros_like(gu)

    def rows_of(q, c):
        return pl.ds(pl.multiple_of((q * 2 + c) * block, block), block)

    def core_copy(i, q):
        return pltpu.make_async_remote_copy(
            src_ref=part.at[i, rows_of(q, other)], dst_ref=core_in.at[i, q],
            send_sem=core_sem.at[0, i, q], recv_sem=core_sem.at[1, i, q],
            device_id={"dp": group * 2 + other}, device_id_type=MESH)

    def chip_copy(i, d):
        to = lax.rem(group + d, groups)
        return pltpu.make_async_remote_copy(
            src_ref=part.at[i, rows_of(to, core)], dst_ref=chip_in.at[i, d - 1],
            send_sem=chip_sem.at[0, i, d - 1], recv_sem=chip_sem.at[1, i, d - 1],
            device_id={"dp": to * 2 + core}, device_id_type=MESH)

    def forward_chip(i):
        for q in range(groups):
            core_copy(i, q).wait()
        for d in range(groups):
            q = lax.rem(group + d, groups)
            part[i, rows_of(q, core)] += core_in[i, q]
            if d:
                chip_copy(i, d).start()

    def wide(a):
        return jnp.concatenate([a] * (tile // LANES), axis=1)

    def backward(i, _):
        a = wide(acc_s[...]) * e_s[i].astype(jnp.float32)
        b = wide(acc_t[...]) * e_t[i].astype(jnp.float32)
        g = (a - b).astype(jnp.bfloat16)
        w = ps[i]
        gw = jnp.dot(zst[...], g, preferred_element_type=jnp.float32)
        wf = w.astype(jnp.float32)
        part[i] = (gw - wf * jnp.sum(wf * gw, axis=0, keepdims=True)) * inv_col[i]
        for q in range(groups):
            core_copy(i, q).start()
        gu[...] += lax.dot_general(g, w, (((1,), (1,)), ((), ())), preferred_element_type=jnp.float32)

        @pl.when(i >= LAG)
        def _():
            forward_chip(i - LAG)
        return 0

    lax.fori_loop(0, steps, backward, 0)

    g_all = gu[...]
    zu = z_unit[...]
    dots = jnp.sum(zu * g_all, axis=1, keepdims=True)
    gu[...] = (g_all - zu * dots) * inv_row[:, 0:1]

    def piece_of(j):
        return pl.ds(pl.multiple_of(j * piece, piece), piece)

    def rs_copy(d):
        to = lax.rem(mp + d, n_mp)
        return pltpu.make_async_remote_copy(
            src_ref=gu.at[piece_of(to)], dst_ref=gu_in.at[d], send_sem=rs_sem.at[0, d], recv_sem=rs_sem.at[1, d],
            device_id={"mp": to}, device_id_type=MESH)

    def ag_copy(d):
        return pltpu.make_async_remote_copy(
            src_ref=gu_in.at[0], dst_ref=gu_all.at[d], send_sem=ag_sem.at[0, d], recv_sem=ag_sem.at[1, d],
            device_id={"mp": lax.rem(mp + d, n_mp)}, device_id_type=MESH)

    for d in range(1, n_mp):
        rs_copy(d).start()

    def tail(i, _):
        forward_chip(i)
        return 0

    lax.fori_loop(max(steps - LAG, 0), steps, tail, 0)

    def store(i):
        cols = pl.ds(pl.multiple_of(i * tile, tile), tile)
        return pltpu.make_async_copy(part.at[i, rows_of(group, core)], protos_hbm.at[:, cols], store_sem.at[i])

    def drain(i, _):
        own = part[i, rows_of(group, core)]
        for d in range(1, groups):
            chip_copy(i, d).wait()
            own = own + chip_in[i, d - 1]
        part[i, rows_of(group, core)] = own
        store(i).start()
        return 0

    early = steps * 5 // 8
    lax.fori_loop(0, early, drain, 0)

    mine = gu[piece_of(mp)]
    for d in range(1, n_mp):
        rs_copy(d).wait()
        mine = mine + gu_in[d]
    gu_in[0] = mine
    for d in range(1, n_mp):
        ag_copy(d).start()
    rows_out[piece_of(mp)] = mine

    lax.fori_loop(early, steps, drain, 0)

    for d in range(1, n_mp):
        ag_copy(d).wait()
        rows_out[piece_of(lax.rem(mp - d + n_mp, n_mp))] = gu_all[d]

    def stored(i, _):
        store(i).wait()
        return 0

    lax.fori_loop(0, steps, stored, 0)


def solution(mesh):
    n_dp, n_mp = mesh.shape["dp"], mesh.shape["mp"]
    groups = n_dp // 2

    def local(student_rows, teacher_rows, student_protos, teacher_protos, center, row_weight):
        rows, feats = student_rows.shape
        cols = student_protos.shape[1]
        tile = math.gcd(cols, 512)
        steps = cols // tile
        block, piece = feats // n_dp, rows // n_mp
        f32, bf16 = jnp.float32, jnp.bfloat16
        vmem, anywhere = pl.BlockSpec(memory_space=pltpu.VMEM), pl.BlockSpec(memory_space=pl.ANY)
        dma = pltpu.SemaphoreType.DMA
        return pl.pallas_call(
            functools.partial(kernel, n_dp, n_mp, tile),
            name="head_backward",
            out_shape=(jax.ShapeDtypeStruct((rows, feats), f32), jax.ShapeDtypeStruct((block, cols), f32)),
            in_specs=[vmem, vmem, anywhere, anywhere, vmem, vmem],
            out_specs=(vmem, anywhere),
            scratch_shapes=[
                pltpu.VMEM((steps, feats, tile), bf16),
                pltpu.VMEM((steps, feats, tile), bf16),
                pltpu.VMEM((steps, rows, tile), bf16),
                pltpu.VMEM((steps, rows, tile), bf16),
                pltpu.VMEM((rows, feats), bf16),
                pltpu.VMEM((rows, feats), bf16),
                pltpu.VMEM((feats, rows), bf16),
                pltpu.VMEM((steps, 1, tile), f32),
                pltpu.VMEM((rows, LANES), f32),
                pltpu.VMEM((rows, feats), f32),
                pltpu.VMEM((rows, LANES), f32),
                pltpu.VMEM((rows, LANES), f32),
                pltpu.VMEM((2, rows), f32),
                pltpu.VMEM((n_mp, 2, rows), f32),
                pltpu.VMEM((rows, feats), f32),
                pltpu.VMEM((n_mp, piece, feats), f32),
                pltpu.VMEM((n_mp, piece, feats), f32),
                pltpu.VMEM((steps, feats, tile), f32),
                pltpu.VMEM((steps, groups, block, tile), f32),
                pltpu.VMEM((steps, groups - 1, block, tile), f32),
                dma((2, steps)),
                dma((2, n_mp)),
                dma((2, steps, groups)),
                dma((2, steps, groups - 1)),
                dma((steps,)),
                dma((2, n_mp)),
                dma((2, n_mp)),
            ],
            compiler_params=pltpu.CompilerParams(
                collective_id=0, has_side_effects=True, vmem_limit_bytes=67043328),
        )(student_rows, teacher_rows, student_protos, teacher_protos, center[None, :], row_weight[None, :])

    placed = (P("dp", None), P("dp", None), P(None, "mp"), P(None, "mp"), P("mp"), P("dp"))
    return jax.shard_map(
        local, mesh=mesh, in_specs=placed, out_specs=(P("dp", None), P("dp", "mp")), check_vma=False
    )
```
